256 devices in a mesh: req: 16 (over x_hi, y, core), ctx: 16 (over x_lo, z).
Axes of the slice: x: 4 (x_hi: 2, x_lo: 2; x = x_hi * 2 + x_lo), y: 4, z: 8, core: 2. Of those that a mesh axis runs over, the one named last changes fastest.
Arguments:
- queries: bfloat16 [1024, 8192], P(('req', 'ctx')), parts along dimension 0, may hold values from -15 to 15
- new_keys: bfloat16 [1024, 512], P(('req', 'ctx')), parts along dimension 0, may hold values from -9 to 9
- new_values: bfloat16 [1024, 512], P(('req', 'ctx')), parts along dimension 0, may hold values from -6 to 6
- cache_keys: bfloat16 [524288, 512], P(('req', 'ctx')), parts along dimension 0, may hold values from -6 to 6
- cache_values: bfloat16 [524288, 512], P(('req', 'ctx')), parts along dimension 0, may hold values from -6 to 6
- cache_length: int32 [16], P('req'), parts along dimension 0, may hold values from 8192 to 32767
- page_table: int32 [4096], P('req'), parts along dimension 0, may hold values from 0 to 255, each once
Outputs:
- attended: bfloat16 [1024, 8192], P(('req', 'ctx')), parts along dimension 0
The draws below stay inside these ranges and needn't reach their ends.
There are 16 independent parts, one for each index of `req`. The reference program is written for one: setup_inputs(seed, part) draws one part's arguments, and reference() takes and returns one part's arrays. A program takes and returns all parts, laid end to end along the dimension named above; each array names one. Nothing has to cross between parts.
Inputs may be any that keep to these rules, and one draw needn't show every extreme that they name: A permutation: logical page p lies in physical rows page_table[p] * 128 to page_table[p] * 128 + 127.
All inputs are finite; a program needn't handle non-finite values.
Results may differ from the reference program's by a relative error of at most 0.004.
Values may be sent and summed in bfloat16 or wider, within the bound.
No kernel may reach another device: no remote copies, remote signals or barrier semaphores. Data moves between devices by JAX's collectives and lax.ppermute only.
A program may use at most 64 MiB of HBM per device.

```python
import jax
import jax.numpy as jnp
from jax import lax

QH = 64
KVH = 4
HD = 128
GROUP = 16
PAGE = 128
NEW = 64
NPAGES = 256
CACHE = 32768


def draw_queries(key, part):
    values = 3.0 * jax.random.normal(jax.random.fold_in(key, 5), (NEW, QH * HD), jnp.float32)
    values = jnp.clip(values, -15.0, 15.0)
    return values.astype(jnp.bfloat16)


def draw_new_keys(key, part):
    values = 1.6 * jax.random.normal(jax.random.fold_in(key, 9), (NEW, KVH * HD), jnp.float32)
    values = jnp.clip(values, -9.0, 9.0)
    return values.astype(jnp.bfloat16)


def block_levels(stream_key, dims, split, smallest, largest):
    level, own = 1.0, jax.random.fold_in(stream_key, 6)
    for axis_at, blocks in split:
        steps = jnp.exp(jax.random.uniform(jax.random.fold_in(own, axis_at), (blocks,), jnp.float32, smallest / len(split), largest / len(split)))
        level = level * jnp.repeat(steps, dims[axis_at] // blocks).reshape([-1 if axis == axis_at else 1 for axis in range(len(dims))])
    return level


def normal_values(stream_key, extent, deviation, reach, split=(), kind=jnp.bfloat16):
    array = deviation * jax.random.normal(stream_key, extent, jnp.float32)
    if split:
        array = array * block_levels(stream_key, extent, split, -0.22, 0.18)
    return jnp.clip(array, -reach, reach).astype(kind)


def setup_inputs(seed: int = 0, part: int = 0) -> dict:
    key_list = jax.random.split(jax.random.key(seed), 8)
    part_keys = jax.random.split(jax.random.fold_in(key_list[7], part), 8)
    queries = draw_queries(jax.random.fold_in(jax.random.fold_in(key_list[7], part), 71), part)
    new_keys = draw_new_keys(jax.random.fold_in(jax.random.fold_in(key_list[7], part), 71), part)
    new_values = normal_values(part_keys[2], (NEW, KVH * HD), 1.0, 6.0, ((0, 16),))
    cache_keys = normal_values(part_keys[3], (CACHE, KVH * HD), 1.0, 6.0, ((0, 16),))
    cache_values = normal_values(part_keys[4], (CACHE, KVH * HD), 1.0, 6.0, ((0, 16),))
    cache_length = jax.random.randint(part_keys[5], (1,), CACHE // 4, CACHE).astype(jnp.int32)
    page_table = jax.random.permutation(part_keys[6], NPAGES).astype(jnp.int32)
    return {"queries": queries, "new_keys": new_keys, "new_values": new_values, "cache_keys": cache_keys, "cache_values": cache_values, "cache_length": cache_length, "page_table": page_table}


floor_score = -1.0e30


def reference(queries, new_keys, new_values, cache_keys, cache_values, cache_length, page_table):
    length = cache_length[0]
    page_count = page_table.shape[0]
    logical = jnp.zeros((page_count,), jnp.int32).at[page_table].set(jnp.arange(page_count, dtype=jnp.int32))
    cache_pos = (logical[:, None] * PAGE + jnp.arange(PAGE, dtype=jnp.int32)[None, :]).reshape(-1)
    new_pos = length + jnp.arange(NEW, dtype=jnp.int32)
    key_pos = jnp.concatenate([cache_pos, new_pos])
    key_ok = jnp.concatenate([cache_pos < length, jnp.ones((NEW,), bool)])
    allowed = key_ok[None, :] & (key_pos[None, :] <= new_pos[:, None])
    keys = jnp.concatenate([cache_keys, new_keys], 0).reshape(-1, KVH, HD).transpose(1, 0, 2)
    values = jnp.concatenate([cache_values, new_values], 0).reshape(-1, KVH, HD).transpose(1, 0, 2)
    grouped = queries.reshape(NEW, KVH, GROUP, HD).transpose(1, 0, 2, 3)
    scale = HD ** -0.5

    def one_group(operands):
        query_group, key_group, value_group = operands
        scores = jnp.einsum('qgd,nd->qgn', query_group.astype(jnp.float32), key_group.astype(jnp.float32)) * scale
        scores = jnp.where(allowed[:, None, :], scores, floor_score)
        top = jnp.max(scores, axis=2, keepdims=True)
        weights = jnp.where(allowed[:, None, :], jnp.exp(scores - top), 0.0)
        denominator = jnp.sum(weights, axis=2)
        rounded = lax.optimization_barrier(weights.astype(jnp.bfloat16))
        mixed = jnp.einsum('qgn,nd->qgd', rounded.astype(jnp.float32), value_group.astype(jnp.float32))
        return mixed / denominator[..., None]

    result = lax.map(one_group, (grouped, keys, values))
    return result.transpose(1, 0, 2, 3).reshape(NEW, QH * HD).astype(jnp.bfloat16)
```

```python
import functools

import jax
import jax.numpy as jnp
from jax import lax
from jax.experimental import pallas as pl
from jax.experimental.pallas import tpu as pltpu
from jax.sharding import PartitionSpec as P

KVH = 4
HD = 128
PAGE = 128
ROWS = 4
GROUP = 16
HR = ROWS * GROUP
BLOCK = KVH * HR
PAYLOAD = BLOCK + 16
FLOOR = -1e30
NEWPAD = 16
SCALE2 = HD ** (-0.5) * 1.4426950408889634
NT = (((1,), (1,)), ((), ()))
NN = (((1,), (0,)), ((), ()))


def split3(x):
    hi = x.astype(jnp.bfloat16)
    rest = x - hi.astype(jnp.float32)
    mid = rest.astype(jnp.bfloat16)
    low = (rest - mid.astype(jnp.float32)).astype(jnp.bfloat16)
    return [hi.astype(jnp.float32), mid.astype(jnp.float32), low.astype(jnp.float32)]


def lse_tile(rows):
    row = lax.broadcasted_iota(jnp.int32, (16, HD), 0)
    tile = jnp.zeros((16, HD), jnp.float32)
    for j, x in enumerate(rows):
        for part, piece in enumerate(split3(x)):
            tile = jnp.where(row == 2 * part + j, jnp.broadcast_to(piece, (16, HD)), tile)
    return tile.astype(jnp.bfloat16)


def prep_kernel(device_ref, length_ref, table_ref, k_ref, v_ref, nk_ref, nv_ref, k_out, v_out, live_out, nk_out, nv_out):
    pages = k_ref.shape[0] // PAGE
    entries = table_ref.shape[1]
    slot = lax.broadcasted_iota(jnp.int32, (pages, entries), 0) + device_ref[0] * pages
    index = lax.broadcasted_iota(jnp.int32, (pages, entries), 1)
    hit = jnp.broadcast_to(table_ref[...], (pages, entries)) == slot
    logical = jnp.sum(jnp.where(hit, index, 0), axis=1, keepdims=True)
    first = jnp.min(logical, axis=0, keepdims=True)
    spare = nk_ref[0:1, :].astype(jnp.float32)
    for s in range(pages):
        mine = logical[s:s + 1, :]
        use = (mine == first) & (mine * PAGE < length_ref[0])
        spare = jnp.where(use, k_ref[s * PAGE:s * PAGE + 1, :].astype(jnp.float32), spare)
    offset = lax.broadcasted_iota(jnp.int32, (PAGE, 1), 0)
    for s in range(pages):
        rows = slice(s * PAGE, (s + 1) * PAGE)
        live = jnp.broadcast_to(logical[s:s + 1, :], (PAGE, 1)) * PAGE + offset < length_ref[0]
        k_out[rows, :] = jnp.where(live, k_ref[rows, :].astype(jnp.float32), spare).astype(jnp.bfloat16)
        v_out[rows, :] = jnp.where(live, v_ref[rows, :].astype(jnp.float32), 0.0).astype(jnp.bfloat16)
        live_out[rows, :] = jnp.broadcast_to(jnp.where(live, 1.0, 0.0), (PAGE, HD)).astype(jnp.bfloat16)
    nk_out[...] = jnp.zeros_like(nk_out)
    nv_out[...] = jnp.zeros_like(nv_out)
    nk_out[0:ROWS, :] = nk_ref[...]
    nv_out[0:ROWS, :] = nv_ref[...]


def attend_kernel(blocks, nin, zsize, device_ref, *refs):
    q_refs, (k_ref, v_ref, live_ref, nk_ref, nv_ref), o_refs = refs[:nin], refs[nin:nin + 5], refs[nin + 5:-5]
    scores, probs, tops = refs[-5:-3], refs[-3:-1], refs[-1]
    m_rows = len(blocks) * HR
    keys = k_ref.shape[0]
    chunk, tile = 256, 32
    chunks, tiles = keys // chunk, m_rows // tile
    device = device_ref[0]
    x, z = device // zsize, lax.rem(device, zsize)

    row = lax.broadcasted_iota(jnp.int32, (HR, NEWPAD), 0)
    col = lax.broadcasted_iota(jnp.int32, (HR, NEWPAD), 1)
    bias = []
    for _, _, (column, by) in blocks:
        origin = (x if column == 0 else 1 - x) * zsize + lax.rem(z + (by % zsize), zsize)
        ok = (col < ROWS) & (col + (device - origin) * ROWS <= (row & (ROWS - 1)))
        bias.append(jnp.where(ok, 0.0, FLOOR))
    bias = jnp.concatenate(bias, 0)
    ones = jnp.ones((NEWPAD, HD), jnp.bfloat16)
    at = lax.broadcasted_iota(jnp.int32, (HR, HD), 0)
    lane = lax.broadcasted_iota(jnp.int32, (HR, HD), 1)

    def lanes(g):
        return slice(g * HD, (g + 1) * HD)

    def rows(g):
        return slice(g * HR, (g + 1) * HR)

    def load(g):
        q = jnp.concatenate([q_refs[i][w, rows(g), :] for (i, w), _, _ in blocks], 0).astype(jnp.float32) * SCALE2
        hi = q.astype(jnp.bfloat16)
        low = (q - hi.astype(jnp.float32)).astype(jnp.bfloat16)
        q = jnp.concatenate([hi, low], 1)
        nk = nk_ref[:, lanes(g)]
        return q, lax.dot_general(q, jnp.concatenate([nk, nk], 1), NT, preferred_element_type=jnp.float32) + bias

    def qk(g, q, c):
        k = k_ref[c * chunk:(c + 1) * chunk, lanes(g)]
        scores[g % 2][:, c * chunk:(c + 1) * chunk] = lax.dot_general(q, jnp.concatenate([k, k], 1), NT, preferred_element_type=jnp.float32)

    def softmax(g, sn, t):
        part = slice(t * tile, (t + 1) * tile)
        buf = scores[g % 2]
        top = buf[part, 0:HD]
        for c in range(1, keys // HD):
            top = jnp.maximum(top, buf[part, c * HD:(c + 1) * HD])
        top = jnp.maximum(jnp.max(top, axis=1, keepdims=True), jnp.max(sn[part], axis=1, keepdims=True))
        wide = jnp.broadcast_to(top, (tile, HD))
        tops[part, :] = wide
        for c in range(keys // HD):
            probs[g % 2][part, c * HD:(c + 1) * HD] = jnp.exp2(buf[part, c * HD:(c + 1) * HD] - wide).astype(jnp.bfloat16)
        return jnp.exp2(sn[part] - top).astype(jnp.bfloat16)

    def pv(g, pn):
        value = jnp.concatenate([v_ref[:, lanes(g)], live_ref[...]], 1)
        acc = lax.dot_general(probs[g % 2][...], value, NN, preferred_element_type=jnp.float32)
        acc = acc + lax.dot_general(pn, jnp.concatenate([nv_ref[:, lanes(g)], ones], 1), NN, preferred_element_type=jnp.float32)
        total = acc[:, HD:]
        some = total > 0.0
        out = jnp.where(some, acc[:, :HD] / total, 0.0).astype(jnp.bfloat16)
        lse = jnp.where(some, tops[...] + jnp.log2(total), FLOOR)
        eye = at + (g % 2) * HR == lane
        found = []
        for b, (_, (o, w), _) in enumerate(blocks):
            o_refs[o][w, rows(g), :] = out[b * HR:(b + 1) * HR]
            found.append(jnp.sum(jnp.where(eye, lse[b * HR:(b + 1) * HR], 0.0), axis=0, keepdims=True))
        return found

    lse = []
    q, sn = load(0)
    for c in range(chunks):
        qk(0, q, c)
    for g in range(KVH):
        now = sn
        if g + 1 < KVH:
            q, sn = load(g + 1)
        pn = []
        for t in range(max(chunks, tiles)):
            if g + 1 < KVH and t < chunks:
                qk(g + 1, q, t)
            if t < tiles:
                pn.append(softmax(g, now, t))
        lse.append(pv(g, jnp.concatenate(pn, 0)))
    for b, (_, (o, w), _) in enumerate(blocks):
        o_refs[o][w, BLOCK:PAYLOAD, :] = lse_tile([lse[0][b] + lse[1][b], lse[2][b] + lse[3][b]])


VM = pl.BlockSpec(memory_space=pltpu.VMEM)
SM = pl.BlockSpec(memory_space=pltpu.SMEM)


def limit(mib):
    return pltpu.CompilerParams(vmem_limit_bytes=mib << 20)


def prep(device, length, table, k, v, nk, nv):
    keys = k.shape[0]
    shapes = [k.shape, v.shape, (keys, HD), (NEWPAD, KVH * HD), (NEWPAD, KVH * HD)]
    return pl.pallas_call(
        prep_kernel,
        out_shape=[jax.ShapeDtypeStruct(s, jnp.bfloat16) for s in shapes],
        in_specs=[SM, SM] + [VM] * 5,
        out_specs=[VM] * 5,
        compiler_params=limit(14),
        cost_estimate=pl.CostEstimate(flops=4 * keys * KVH * HD, bytes_accessed=8 * keys * KVH * HD, transcendentals=0),
        name="prep",
    )(device, length, table, k, v, nk, nv)


def attend(zsize, device, arrays, blocks, widths, store):
    keys = store[0].shape[0]
    m_rows = len(blocks) * HR
    return pl.pallas_call(
        functools.partial(attend_kernel, blocks, len(arrays), zsize),
        out_shape=[jax.ShapeDtypeStruct((w, PAYLOAD, HD), jnp.bfloat16) for w in widths],
        in_specs=[SM] + [VM] * (len(arrays) + 5),
        out_specs=[VM] * len(widths),
        scratch_shapes=[pltpu.VMEM((m_rows, keys), jnp.float32)] * 2 + [pltpu.VMEM((m_rows, keys), jnp.bfloat16)] * 2 + [pltpu.VMEM((m_rows, HD), jnp.float32)],
        compiler_params=limit(20),
        cost_estimate=pl.CostEstimate(flops=4 * m_rows * KVH * keys * HD, bytes_accessed=4 * keys * KVH * HD, transcendentals=m_rows * KVH * keys),
        name=f"attend{len(blocks)}",
    )(device, *arrays, *store)


def weights_of(tiles):
    n = len(tiles)
    halves = []
    for j in range(2):
        rows = [t[j:j + 1] + (t[2 + j:3 + j] + t[4 + j:5 + j]) for t in tiles]
        top = functools.reduce(jnp.maximum, rows)
        w = [jnp.exp2(r - top) for r in rows]
        total = functools.reduce(jnp.add, w)
        inv = 1.0 / total
        row = lax.broadcasted_iota(jnp.int32, (HD, HD), 0)
        square = jnp.zeros((HD, HD), jnp.float32)
        for i in range(n):
            square = jnp.where(row == i, jnp.broadcast_to(w[i] * inv, (HD, HD)), square)
        halves.append((square.T, top + jnp.log2(total)))
    return halves


def gather_kernel(n, *refs):
    parts, (mine_ref, tile_ref, other_ref) = refs[:n], refs[n:]
    for b in range(2):
        halves = weights_of([p[b, BLOCK:PAYLOAD, :].astype(jnp.float32) for p in parts])
        for j, (cols, _) in enumerate(halves):
            rows = slice(j * HD, (j + 1) * HD)
            acc = None
            for i, p in enumerate(parts):
                term = cols[:, i:i + 1] * p[b, rows, :].astype(jnp.float32)
                acc = term if acc is None else acc + term
            if b == 0:
                mine_ref[rows, :] = acc
            else:
                other_ref[rows, :] = acc.astype(jnp.bfloat16)
        tile = lse_tile([halves[0][1], halves[1][1]])
        if b == 0:
            tile_ref[...] = tile
        else:
            other_ref[BLOCK:PAYLOAD, :] = tile


def gather(parts):
    return pl.pallas_call(
        functools.partial(gather_kernel, len(parts)),
        out_shape=[
            jax.ShapeDtypeStruct((BLOCK, HD), jnp.float32),
            jax.ShapeDtypeStruct((16, HD), jnp.bfloat16),
            jax.ShapeDtypeStruct((PAYLOAD, HD), jnp.bfloat16),
        ],
        in_specs=[VM] * len(parts),
        out_specs=[VM] * 3,
        compiler_params=limit(6),
        name="gather",
    )(*parts)


def final_kernel(mine_ref, tile_ref, got_ref, out_ref):
    halves = weights_of([tile_ref[...].astype(jnp.float32), got_ref[BLOCK:PAYLOAD, :].astype(jnp.float32)])
    for j, (cols, _) in enumerate(halves):
        rows = slice(j * HD, (j + 1) * HD)
        acc = cols[:, 0:1] * mine_ref[rows, :] + cols[:, 1:2] * got_ref[rows, :].astype(jnp.float32)
        out_ref[rows, :] = acc.astype(jnp.bfloat16)


def final(mine, tile, got):
    return pl.pallas_call(
        final_kernel,
        out_shape=jax.ShapeDtypeStruct((BLOCK, HD), jnp.bfloat16),
        in_specs=[VM] * 3,
        out_specs=VM,
        compiler_params=limit(3),
        name="final",
    )(mine, tile, got)


def local(queries, new_keys, new_values, cache_keys, cache_values, cache_length, page_table):
    zsize = lax.axis_size("ctx") // 2

    def zshift(x, by):
        return lax.ppermute(x, "ctx", [(i, (i // zsize) * zsize + (i % zsize + by) % zsize) for i in range(2 * zsize)])

    def xswap(x):
        return lax.ppermute(x, "ctx", [(i, (i + zsize) % (2 * zsize)) for i in range(2 * zsize)])

    device = lax.axis_index("ctx").astype(jnp.int32).reshape(1)
    mine = queries.reshape(ROWS, KVH * GROUP, HD).transpose(1, 0, 2).reshape(BLOCK, HD)
    both = jnp.stack([mine, xswap(mine)])
    store = prep(device, cache_length, page_table.reshape(1, -1), cache_keys, cache_values, new_keys, new_values)

    up, down = both, both
    results = []
    half = zsize // 2
    for k in range(1, half):
        up, down = zshift(up, 1), zshift(down, -1)
        arrays, widths = [up, down], [2, 2]
        blocks = [((i, w), (i, w), (w, by)) for i, by in ((0, -k), (1, k)) for w in range(2)]
        if k == 1:
            arrays, widths = arrays + [both], widths + [2]
            blocks = blocks + [((2, w), (2, w), (w, 0)) for w in range(2)]
        parts = attend(zsize, device, arrays, blocks, widths, store)
        results += [zshift(parts[0], -k), zshift(parts[1], k)] + list(parts[2:])
    far = [zshift(up[0:1], 1), zshift(down[1:2], -1)]
    blocks = [((w, 0), (0, w), (w, half)) for w in range(2)]
    results.append(zshift(attend(zsize, device, far, blocks, [2], store)[0], half))

    kept, tile, sent = gather(results)
    out = final(kept, tile, xswap(sent))
    return out.reshape(KVH * GROUP, ROWS, HD).transpose(1, 0, 2).reshape(ROWS, KVH * GROUP * HD)


def solution(mesh):
    spec = P(("req", "ctx"), None)
    in_specs = (spec, spec, spec, spec, spec, P("req"), P("req"))
    return jax.shard_map(local, mesh=mesh, in_specs=in_specs, out_specs=spec, check_vma=False)
```

```python
import functools

import jax
import jax.numpy as jnp
from jax import lax
from jax.experimental import pallas as pl
from jax.experimental.pallas import tpu as pltpu
from jax.sharding import PartitionSpec as P


KVH = 4
HD = 128
PAGE = 128
ROWS = 4
GROUP = 16
HR = ROWS * GROUP
BLOCK = KVH * HR
PAYLOAD = BLOCK + 16
KEPT = BLOCK + 8
FLOOR = -1e30
NEWPAD = 16
SCALE2 = HD ** (-0.5) * 1.4426950408889634
NT = (((1,), (1,)), ((), ()))
NN = (((1,), (0,)), ((), ()))


def split3(x):
    hi = x.astype(jnp.bfloat16)
    rest = x - hi.astype(jnp.float32)
    mid = rest.astype(jnp.bfloat16)
    low = (rest - mid.astype(jnp.float32)).astype(jnp.bfloat16)
    return [hi.astype(jnp.float32), mid.astype(jnp.float32), low.astype(jnp.float32)]


def lse_tile(rows):
    row = lax.broadcasted_iota(jnp.int32, (16, HD), 0)
    tile = jnp.zeros((16, HD), jnp.float32)
    for j, x in enumerate(rows):
        for part, piece in enumerate(split3(x)):
            tile = jnp.where(row == 2 * part + j, jnp.broadcast_to(piece, (16, HD)), tile)
    return tile.astype(jnp.bfloat16)


def prep_kernel(device_ref, length_ref, table_ref, k_hbm, v_hbm, nk_ref, nv_ref, k_out, v_out, live_out, nk_out, nv_out, k_ref, v_ref, sems):
    pages = k_ref.shape[0] // PAGE
    pieces = sems.shape[0] // 2
    size = k_ref.shape[0] // pieces
    copies = []
    for src, dst, base in ((v_hbm, v_ref, 0), (k_hbm, k_ref, pieces)):
        for i in range(pieces):
            at = pl.ds(i * size, size)
            copies.append(pltpu.make_async_copy(src.at[at], dst.at[at], sems.at[base + i]))
            copies[-1].start()
    entries = table_ref.shape[1]
    slot = lax.broadcasted_iota(jnp.int32, (pages, entries), 0) + device_ref[0] * pages
    index = lax.broadcasted_iota(jnp.int32, (pages, entries), 1)
    hit = jnp.broadcast_to(table_ref[...], (pages, entries)) == slot
    logical = jnp.sum(jnp.where(hit, index, 0), axis=1, keepdims=True)
    first = jnp.min(logical, axis=0, keepdims=True)
    offset = lax.broadcasted_iota(jnp.int32, (PAGE, 1), 0)
    nk_out[...] = jnp.zeros_like(nk_out)
    nv_out[...] = jnp.zeros_like(nv_out)
    nk_out[0:ROWS, :] = nk_ref[...]
    nv_out[0:ROWS, :] = nv_ref[...]

    def live_of(s):
        return jnp.broadcast_to(logical[s:s + 1, :], (PAGE, 1)) * PAGE + offset < length_ref[0]

    for s in range(pages):
        if s % (pages // pieces) == 0:
            copies[s // (pages // pieces)].wait()
        rows = slice(s * PAGE, (s + 1) * PAGE)
        live = live_of(s)
        v_out[rows, :] = jnp.where(live, v_ref[rows, :].astype(jnp.float32), 0.0).astype(jnp.bfloat16)
        live_out[rows, :] = jnp.broadcast_to(jnp.where(live, 1.0, 0.0), (PAGE, HD)).astype(jnp.bfloat16)
    for copy in copies[pieces:]:
        copy.wait()
    spare = nk_ref[0:1, :].astype(jnp.float32)
    for s in range(pages):
        mine = logical[s:s + 1, :]
        use = (mine == first) & (mine * PAGE < length_ref[0])
        spare = jnp.where(use, k_ref[s * PAGE:s * PAGE + 1, :].astype(jnp.float32), spare)
    for s in range(pages):
        rows = slice(s * PAGE, (s + 1) * PAGE)
        k_out[rows, :] = jnp.where(live_of(s), k_ref[rows, :].astype(jnp.float32), spare).astype(jnp.bfloat16)


def attend_kernel(blocks, nin, zsize, device_ref, *refs):
    q_refs, (k_ref, v_ref, live_ref, nk_ref, nv_ref) = refs[:nin], refs[nin:nin + 5]
    keep_ref, send_ref = refs[-7:-5]
    scores, probs, tops = refs[-5:-3], refs[-3:-1], refs[-1]
    m_rows = len(blocks) * HR
    keys = k_ref.shape[0]
    chunk, tile = 256, 32
    chunks, tiles = keys // chunk, m_rows // tile
    device = device_ref[0]
    x, z = device // zsize, lax.rem(device, zsize)

    row = lax.broadcasted_iota(jnp.int32, (HR, NEWPAD), 0)
    col = lax.broadcasted_iota(jnp.int32, (HR, NEWPAD), 1)
    bias = []
    for _, _, (column, by) in blocks:
        origin = (x if column == 0 else 1 - x) * zsize + lax.rem(z + (by % zsize), zsize)
        ok = (col < ROWS) & (col + (device - origin) * ROWS <= (row & (ROWS - 1)))
        bias.append(jnp.where(ok, 0.0, FLOOR))
    bias = jnp.concatenate(bias, 0)
    ones = jnp.ones((NEWPAD, HD), jnp.bfloat16)
    at = lax.broadcasted_iota(jnp.int32, (HR, HD), 0)
    lane = lax.broadcasted_iota(jnp.int32, (HR, HD), 1)

    def lanes(g):
        return slice(g * HD, (g + 1) * HD)

    def rows(g):
        return slice(g * HR, (g + 1) * HR)

    def load(g):
        q = jnp.concatenate([q_refs[i][w, rows(g), :] for (i, w), _, _ in blocks], 0).astype(jnp.float32) * SCALE2
        hi = q.astype(jnp.bfloat16)
        low = (q - hi.astype(jnp.float32)).astype(jnp.bfloat16)
        q = jnp.concatenate([hi, low], 1)
        nk = nk_ref[:, lanes(g)]
        return q, lax.dot_general(q, jnp.concatenate([nk, nk], 1), NT, preferred_element_type=jnp.float32) + bias

    def qk(g, q, c):
        k = k_ref[c * chunk:(c + 1) * chunk, lanes(g)]
        scores[g % 2][:, c * chunk:(c + 1) * chunk] = lax.dot_general(q, jnp.concatenate([k, k], 1), NT, preferred_element_type=jnp.float32)

    def softmax(g, sn, t):
        part = slice(t * tile, (t + 1) * tile)
        buf = scores[g % 2]
        top = buf[part, 0:HD]
        for c in range(1, keys // HD):
            top = jnp.maximum(top, buf[part, c * HD:(c + 1) * HD])
        top = jnp.maximum(jnp.max(top, axis=1, keepdims=True), jnp.max(sn[part], axis=1, keepdims=True))
        wide = jnp.broadcast_to(top, (tile, HD))
        tops[part, :] = wide
        for c in range(keys // HD):
            probs[g % 2][part, c * HD:(c + 1) * HD] = jnp.exp2(buf[part, c * HD:(c + 1) * HD] - wide).astype(jnp.bfloat16)
        return jnp.exp2(sn[part] - top).astype(jnp.bfloat16)

    def pv(g, pn):
        value = jnp.concatenate([v_ref[:, lanes(g)], live_ref[...]], 1)
        acc = lax.dot_general(probs[g % 2][...], value, NN, preferred_element_type=jnp.float32)
        acc = acc + lax.dot_general(pn, jnp.concatenate([nv_ref[:, lanes(g)], ones], 1), NN, preferred_element_type=jnp.float32)
        total = acc[:, HD:]
        some = total > 0.0
        out = jnp.where(some, acc[:, :HD] / total, 0.0)
        lse = jnp.where(some, tops[...] + jnp.log2(total), FLOOR)
        eye = at + (g % 2) * HR == lane
        found = []
        for b, (_, place, (column, _)) in enumerate(blocks):
            if column == 0:
                keep_ref[place, rows(g), :] = out[b * HR:(b + 1) * HR]
            else:
                send_ref[place, rows(g), :] = out[b * HR:(b + 1) * HR].astype(jnp.bfloat16)
            found.append(jnp.sum(jnp.where(eye, lse[b * HR:(b + 1) * HR], 0.0), axis=0, keepdims=True))
        return found

    lse = []
    q, sn = load(0)
    for c in range(chunks):
        qk(0, q, c)
    for g in range(KVH):
        now = sn
        if g + 1 < KVH:
            q, sn = load(g + 1)
        pn = []
        for t in range(max(chunks, tiles)):
            if g + 1 < KVH and t < chunks:
                qk(g + 1, q, t)
            if t < tiles:
                pn.append(softmax(g, now, t))
        lse.append(pv(g, jnp.concatenate(pn, 0)))
    for b, (_, place, (column, _)) in enumerate(blocks):
        found = [lse[0][b] + lse[1][b], lse[2][b] + lse[3][b]]
        if column == 0:
            for j in range(2):
                keep_ref[place, BLOCK + j:BLOCK + j + 1, :] = found[j]
        else:
            send_ref[place, BLOCK:PAYLOAD, :] = lse_tile(found)


VM = pl.BlockSpec(memory_space=pltpu.VMEM)
SM = pl.BlockSpec(memory_space=pltpu.SMEM)


def limit(mib):
    return pltpu.CompilerParams(vmem_limit_bytes=mib << 20)


def prep(device, length, table, k, v, nk, nv):
    keys = k.shape[0]
    shapes = [k.shape, v.shape, (keys, HD), (NEWPAD, KVH * HD), (NEWPAD, KVH * HD)]
    hbm = pl.BlockSpec(memory_space=pltpu.HBM)
    return pl.pallas_call(
        prep_kernel,
        out_shape=[jax.ShapeDtypeStruct(s, jnp.bfloat16) for s in shapes],
        in_specs=[SM, SM, VM, hbm, hbm, VM, VM],
        out_specs=[VM] * 5,
        scratch_shapes=[pltpu.VMEM(k.shape, jnp.bfloat16), pltpu.VMEM(v.shape, jnp.bfloat16), pltpu.SemaphoreType.DMA((8,))],
        compiler_params=limit(48),
        cost_estimate=pl.CostEstimate(flops=4 * keys * KVH * HD, bytes_accessed=8 * keys * KVH * HD, transcendentals=0),
        name="prep",
    )(device, length, table, k, v, nk, nv)


def attend(zsize, device, arrays, blocks, store, total, before=None):
    keys = store[0].shape[0]
    m_rows = len(blocks) * HR
    kept = sum(column == 0 for _, _, (column, _) in blocks)
    extra = [] if before is None else [before]
    return pl.pallas_call(
        functools.partial(attend_kernel, blocks, len(arrays), zsize),
        out_shape=[jax.ShapeDtypeStruct((kept, KEPT, HD), jnp.float32), jax.ShapeDtypeStruct((total, PAYLOAD, HD), jnp.bfloat16)],
        in_specs=[SM] + [VM] * (len(arrays) + 5 + len(extra)),
        out_specs=[VM] * 2,
        scratch_shapes=[pltpu.VMEM((m_rows, keys), jnp.float32)] * 2 + [pltpu.VMEM((m_rows, keys), jnp.bfloat16)] * 2 + [pltpu.VMEM((m_rows, HD), jnp.float32)],
        input_output_aliases={6 + len(arrays): 1} if extra else {},
        compiler_params=limit(20),
        cost_estimate=pl.CostEstimate(flops=4 * m_rows * KVH * keys * HD, bytes_accessed=4 * keys * KVH * HD, transcendentals=m_rows * KVH * keys),
    )(device, *arrays, *store, *extra)


def columns(rows):
    row = lax.broadcasted_iota(jnp.int32, (HD, HD), 0)
    square = jnp.zeros((HD, HD), jnp.float32)
    for i, x in enumerate(rows):
        square = jnp.where(row == i, jnp.broadcast_to(x, (HD, HD)), square)
    return square.T


def lse_rows(ref):
    tile = ref[BLOCK:PAYLOAD, :].astype(jnp.float32)
    return [tile[j:j + 1] + (tile[2 + j:3 + j] + tile[4 + j:5 + j]) for j in range(2)]


def shares(rows):
    top = functools.reduce(jnp.maximum, rows)
    w = [jnp.exp2(r - top) for r in rows]
    total = functools.reduce(jnp.add, w)
    inv = 1.0 / total
    return [x * inv for x in w], top + jnp.log2(total)


def pair_kernel(counts, own, *refs):
    keeps, got_ref, outs = refs[:len(counts)], refs[len(counts)], refs[len(counts) + 1:]
    places = [(keep, i) for keep, n in zip(keeps, counts) for i in range(n)]
    rows, lses = [], []
    for p, (keep, i) in enumerate(places):
        theirs = lse_rows(got_ref.at[p])
        lses.append([])
        for j in range(2):
            w, lse = shares([keep[i, BLOCK + j:BLOCK + j + 1, :], theirs[j]])
            rows += w
            lses[-1].append(lse)
    cols = columns(rows)
    for p, (keep, i) in enumerate(places):
        for j in range(2):
            at, c = slice(j * HD, (j + 1) * HD), 4 * p + 2 * j
            acc = cols[:, c:c + 1] * keep[i, at, :] + cols[:, c + 1:c + 2] * got_ref[p, at, :].astype(jnp.float32)
            outs[p][at, :] = acc.astype(outs[p].dtype)
            if own and p == 0:
                outs[p][BLOCK + j:BLOCK + j + 1, :] = lses[p][j]
        if not (own and p == 0):
            outs[p][BLOCK:PAYLOAD, :] = lse_tile(lses[p])


def pair(keeps, got, own):
    counts = [k.shape[0] for k in keeps]
    shapes = [jax.ShapeDtypeStruct((PAYLOAD, HD), jnp.bfloat16)] * sum(counts)
    if own:
        shapes[0] = jax.ShapeDtypeStruct((KEPT, HD), jnp.float32)
    return pl.pallas_call(
        functools.partial(pair_kernel, counts, own),
        out_shape=shapes,
        in_specs=[VM] * (len(keeps) + 1),
        out_specs=[VM] * len(shapes),
        compiler_params=limit(4),
    )(*keeps, got)


def final_kernel(n, own_ref, *refs):
    parts, out_ref = refs[:n], refs[n]
    theirs = [lse_rows(p) for p in parts]
    for j in range(2):
        at = slice(j * HD, (j + 1) * HD)
        w, _ = shares([own_ref[BLOCK + j:BLOCK + j + 1, :]] + [t[j] for t in theirs])
        cols = columns(w)
        acc = cols[:, 0:1] * own_ref[at, :]
        for i, p in enumerate(parts):
            acc = acc + cols[:, i + 1:i + 2] * p[at, :].astype(jnp.float32)
        out_ref[at, :] = acc.astype(jnp.bfloat16)


def final(own, parts):
    return pl.pallas_call(
        functools.partial(final_kernel, len(parts)),
        out_shape=jax.ShapeDtypeStruct((BLOCK, HD), jnp.bfloat16),
        in_specs=[VM] * (1 + len(parts)),
        out_specs=VM,
        compiler_params=limit(4),
        name="final",
    )(own, *parts)


def local(queries, new_keys, new_values, cache_keys, cache_values, cache_length, page_table):
    zsize = lax.axis_size("ctx") // 2
    half = zsize // 2

    def zshift(x, by):
        return lax.ppermute(x, "ctx", [(i, (i // zsize) * zsize + (i % zsize + by) % zsize) for i in range(2 * zsize)])

    def xswap(x):
        return lax.ppermute(x, "ctx", [(i, (i + zsize) % (2 * zsize)) for i in range(2 * zsize)])

    def blocks_at(k, base):
        return [((i, w), (base if w else 0) + i, (w, by)) for i, by in ((0, -k), (1, k)) for w in range(2)]

    device = lax.axis_index("ctx").astype(jnp.int32).reshape(1)
    mine = queries.reshape(ROWS, KVH * GROUP, HD).transpose(1, 0, 2).reshape(BLOCK, HD)
    store = prep(device, cache_length, page_table.reshape(1, -1), cache_keys, cache_values, new_keys, new_values)
    swapped, store = lax.optimization_barrier((xswap(mine), store))
    both = jnp.stack([mine, swapped])

    near = 2 * half - 3
    run = functools.partial(attend, zsize, device)
    keeps = []
    keep, send = run([both], [((0, w), 0, (w, 0)) for w in range(2)], store, near)
    keeps.append(keep)
    up, down = both, both
    for k in range(1, half - 1):
        up, down, send = lax.optimization_barrier((zshift(up, 1), zshift(down, -1), send))
        keep, send = run([up, down], blocks_at(k, 2 * k - 1), store, near, send)
        keeps.append(keep)
    up, down, send = lax.optimization_barrier((zshift(up, 1), zshift(down, -1), send))
    far = (zshift(up[0:1], 1), zshift(down[1:2], -1))
    far_keep, far_send = run([up, down], blocks_at(half - 1, 0), store, 3)
    far, far_send = lax.optimization_barrier((far, far_send))
    last_keep, far_send = run(list(far), [((0, 0), 0, (0, half)), ((1, 0), 2, (1, half))], store, 3, far_send)

    got, far_got = xswap(send), xswap(far_send)
    own, *out = pair(keeps, got, True)
    far_out = pair([far_keep, last_keep], far_got, False)
    back = [zshift(far_out[2], half), zshift(far_out[0], 1 - half), zshift(far_out[1], half - 1)]
    for k in range(half - 2, 0, -1):
        back += [zshift(out[2 * k - 2], -k), zshift(out[2 * k - 1], k)]
    out = final(own, back)
    return out.reshape(KVH * GROUP, ROWS, HD).transpose(1, 0, 2).reshape(ROWS, KVH * GROUP * HD)


def solution(mesh):
    spec = P(("req", "ctx"), None)
    in_specs = (spec, spec, spec, spec, spec, P("req"), P("req"))

    return jax.shard_map(local, mesh=mesh, in_specs=in_specs, out_specs=spec, check_vma=False)
```

```python
import functools

import jax
import jax.numpy as jnp
from jax import lax
from jax.experimental import pallas as pl
from jax.experimental.pallas import tpu as pltpu
from jax.sharding import PartitionSpec as P


KVH = 4
HD = 128
PAGE = 128
ROWS = 4
GROUP = 16
HR = ROWS * GROUP
BLOCK = KVH * HR
PAYLOAD = BLOCK + 16
KEPT = BLOCK + 8
FLOOR = -1e30
NEWPAD = 16
SCALE2 = HD ** (-0.5) * 1.4426950408889634
NT = (((1,), (1,)), ((), ()))
NN = (((1,), (0,)), ((), ()))


def split3(x):
    hi = x.astype(jnp.bfloat16)
    rest = x - hi.astype(jnp.float32)
    mid = rest.astype(jnp.bfloat16)
    low = (rest - mid.astype(jnp.float32)).astype(jnp.bfloat16)
    return [hi.astype(jnp.float32), mid.astype(jnp.float32), low.astype(jnp.float32)]


def lse_tile(rows):
    row = lax.broadcasted_iota(jnp.int32, (16, HD), 0)
    tile = jnp.zeros((16, HD), jnp.float32)
    for j, x in enumerate(rows):
        for part, piece in enumerate(split3(x)):
            tile = jnp.where(row == 2 * part + j, jnp.broadcast_to(piece, (16, HD)), tile)
    return tile.astype(jnp.bfloat16)


def live_pages(device_ref, meta_ref, pages):
    entries = meta_ref.shape[1] - HD
    length = meta_ref[:, entries:entries + 1]
    slot = lax.broadcasted_iota(jnp.int32, (pages, entries), 0) + device_ref[0] * pages
    index = lax.broadcasted_iota(jnp.int32, (pages, entries), 1)
    hit = jnp.broadcast_to(meta_ref[:, 0:entries], (pages, entries)) == slot
    logical = jnp.sum(jnp.where(hit, index, 0), axis=1, keepdims=True)
    offset = lax.broadcasted_iota(jnp.int32, (PAGE, 1), 0)
    return logical, length, lambda s: jnp.broadcast_to(logical[s:s + 1, :], (PAGE, 1)) * PAGE + offset < length


def fetch(hbm, ref, sems):
    size = ref.shape[0] // sems.shape[0]
    copies = []
    for i in range(sems.shape[0]):
        at = pl.ds(i * size, size)
        copies.append(pltpu.make_async_copy(hbm.at[at], ref.at[at], sems.at[i]))
        copies[-1].start()
    return copies


def prep_keys_kernel(device_ref, meta_ref, new_ref, k_hbm, k_out, nk_out, nv_out, k_ref, sems):
    copies = fetch(k_hbm, k_ref, sems)
    pages = k_ref.shape[0] // PAGE
    logical, length, live = live_pages(device_ref, meta_ref, pages)
    first = jnp.min(logical, axis=0, keepdims=True)
    nk_out[...] = jnp.zeros_like(nk_out)
    nv_out[...] = jnp.zeros_like(nv_out)
    nk_out[0:ROWS, :] = new_ref[0:ROWS, :]
    nv_out[0:ROWS, :] = new_ref[ROWS:2 * ROWS, :]
    spare = new_ref[0:1, :].astype(jnp.float32)
    for copy in copies:
        copy.wait()
    for s in range(pages):
        mine = logical[s:s + 1, :]
        use = (mine == first) & (mine * PAGE < length)
        spare = jnp.where(use, k_ref[s * PAGE:s * PAGE + 1, :].astype(jnp.float32), spare)
    for s in range(pages):
        rows = slice(s * PAGE, (s + 1) * PAGE)
        k_out[rows, :] = jnp.where(live(s), k_ref[rows, :].astype(jnp.float32), spare).astype(jnp.bfloat16)


def prep_values_kernel(device_ref, meta_ref, v_hbm, v_out, live_out, v_ref, sems):
    copies = fetch(v_hbm, v_ref, sems)
    pages = v_ref.shape[0] // PAGE
    _, _, live = live_pages(device_ref, meta_ref, pages)
    for s in range(pages):
        if s % (pages // len(copies)) == 0:
            copies[s // (pages // len(copies))].wait()
        rows = slice(s * PAGE, (s + 1) * PAGE)
        ok = live(s)
        v_out[rows, :] = jnp.where(ok, v_ref[rows, :].astype(jnp.float32), 0.0).astype(jnp.bfloat16)
        live_out[rows, :] = jnp.broadcast_to(jnp.where(ok, 1.0, 0.0), (PAGE, HD)).astype(jnp.bfloat16)


def attend_kernel(blocks, nin, zsize, device_ref, *refs):
    q_refs, (k_ref, v_ref, live_ref, nk_ref, nv_ref) = refs[:nin], refs[nin:nin + 5]
    keep_ref, send_ref = refs[-7:-5]
    scores, probs, tops = refs[-5:-3], refs[-3:-1], refs[-1]
    m_rows = len(blocks) * HR
    keys = k_ref.shape[0]
    chunk, tile = 256, 32
    chunks, tiles = keys // chunk, m_rows // tile
    device = device_ref[0]
    x, z = device // zsize, lax.rem(device, zsize)

    row = lax.broadcasted_iota(jnp.int32, (HR, NEWPAD), 0)
    col = lax.broadcasted_iota(jnp.int32, (HR, NEWPAD), 1)
    bias = []
    for _, _, (column, by) in blocks:
        origin = (x if column == 0 else 1 - x) * zsize + lax.rem(z + (by % zsize), zsize)
        ok = (col < ROWS) & (col + (device - origin) * ROWS <= (row & (ROWS - 1)))
        bias.append(jnp.where(ok, 0.0, FLOOR))
    bias = jnp.concatenate(bias, 0)
    ones = jnp.ones((NEWPAD, HD), jnp.bfloat16)
    at = lax.broadcasted_iota(jnp.int32, (HR, HD), 0)
    lane = lax.broadcasted_iota(jnp.int32, (HR, HD), 1)

    def lanes(g):
        return slice(g * HD, (g + 1) * HD)

    def rows(g):
        return slice(g * HR, (g + 1) * HR)

    def load(g):
        q = jnp.concatenate([q_refs[i][w, rows(g), :] for (i, w), _, _ in blocks], 0).astype(jnp.float32) * SCALE2
        hi = q.astype(jnp.bfloat16)
        low = (q - hi.astype(jnp.float32)).astype(jnp.bfloat16)
        q = jnp.concatenate([hi, low], 1)
        nk = nk_ref[:, lanes(g)]
        return q, lax.dot_general(q, jnp.concatenate([nk, nk], 1), NT, preferred_element_type=jnp.float32) + bias

    def qk(g, q, c):
        k = k_ref[c * chunk:(c + 1) * chunk, lanes(g)]
        scores[g % 2][:, c * chunk:(c + 1) * chunk] = lax.dot_general(q, jnp.concatenate([k, k], 1), NT, preferred_element_type=jnp.float32)

    def softmax(g, sn, t):
        part = slice(t * tile, (t + 1) * tile)
        buf = scores[g % 2]
        top = buf[part, 0:HD]
        for c in range(1, keys // HD):
            top = jnp.maximum(top, buf[part, c * HD:(c + 1) * HD])
        top = jnp.maximum(jnp.max(top, axis=1, keepdims=True), jnp.max(sn[part], axis=1, keepdims=True))
        wide = jnp.broadcast_to(top, (tile, HD))
        tops[part, :] = wide
        for c in range(keys // HD):
            probs[g % 2][part, c * HD:(c + 1) * HD] = jnp.exp2(buf[part, c * HD:(c + 1) * HD] - wide).astype(jnp.bfloat16)
        return jnp.exp2(sn[part] - top).astype(jnp.bfloat16)

    def pv(g, pn):
        value = jnp.concatenate([v_ref[:, lanes(g)], live_ref[...]], 1)
        acc = lax.dot_general(probs[g % 2][...], value, NN, preferred_element_type=jnp.float32)
        acc = acc + lax.dot_general(pn, jnp.concatenate([nv_ref[:, lanes(g)], ones], 1), NN, preferred_element_type=jnp.float32)
        total = acc[:, HD:]
        some = total > 0.0
        out = jnp.where(some, acc[:, :HD] / total, 0.0)
        lse = jnp.where(some, tops[...] + jnp.log2(total), FLOOR)
        eye = at + (g % 2) * HR == lane
        found = []
        for b, (_, place, (column, _)) in enumerate(blocks):
            if column == 0:
                keep_ref[place, rows(g), :] = out[b * HR:(b + 1) * HR]
            else:
                send_ref[place, rows(g), :] = out[b * HR:(b + 1) * HR].astype(jnp.bfloat16)
            found.append(jnp.sum(jnp.where(eye, lse[b * HR:(b + 1) * HR], 0.0), axis=0, keepdims=True))
        return found

    lse = []
    q, sn = load(0)
    for c in range(chunks):
        qk(0, q, c)
    for g in range(KVH):
        now = sn
        if g + 1 < KVH:
            q, sn = load(g + 1)
        pn = []
        for t in range(max(chunks, tiles)):
            if g + 1 < KVH and t < chunks:
                qk(g + 1, q, t)
            if t < tiles:
                pn.append(softmax(g, now, t))
        lse.append(pv(g, jnp.concatenate(pn, 0)))
    for b, (_, place, (column, _)) in enumerate(blocks):
        found = [lse[0][b] + lse[1][b], lse[2][b] + lse[3][b]]
        if column == 0:
            for j in range(2):
                keep_ref[place, BLOCK + j:BLOCK + j + 1, :] = found[j]
        else:
            send_ref[place, BLOCK:PAYLOAD, :] = lse_tile(found)


VM = pl.BlockSpec(memory_space=pltpu.VMEM)
SM = pl.BlockSpec(memory_space=pltpu.SMEM)


def limit(mib):
    return pltpu.CompilerParams(vmem_limit_bytes=mib << 20)


def prep(kernel, device, small, big, shapes, mib):
    return pl.pallas_call(
        kernel,
        out_shape=[jax.ShapeDtypeStruct(s, jnp.bfloat16) for s in shapes],
        in_specs=[SM] + [VM] * len(small) + [pl.BlockSpec(memory_space=pltpu.HBM)],
        out_specs=[VM] * len(shapes),
        scratch_shapes=[pltpu.VMEM(big.shape, jnp.bfloat16), pltpu.SemaphoreType.DMA((4,))],
        compiler_params=limit(mib),
        cost_estimate=pl.CostEstimate(flops=4 * big.size, bytes_accessed=4 * big.size, transcendentals=0),
    )(device, *small, big)


def attend(zsize, device, arrays, blocks, store, total, before=None):
    keys = store[0].shape[0]
    m_rows = len(blocks) * HR
    kept = sum(column == 0 for _, _, (column, _) in blocks)
    extra = [] if before is None else [before]
    return pl.pallas_call(
        functools.partial(attend_kernel, blocks, len(arrays), zsize),
        out_shape=[jax.ShapeDtypeStruct((kept, KEPT, HD), jnp.float32), jax.ShapeDtypeStruct((total, PAYLOAD, HD), jnp.bfloat16)],
        in_specs=[SM] + [VM] * (len(arrays) + 5 + len(extra)),
        out_specs=[VM] * 2,
        scratch_shapes=[pltpu.VMEM((m_rows, keys), jnp.float32)] * 2 + [pltpu.VMEM((m_rows, keys), jnp.bfloat16)] * 2 + [pltpu.VMEM((m_rows, HD), jnp.float32)],
        input_output_aliases={6 + len(arrays): 1} if extra else {},
        compiler_params=limit(20),
        cost_estimate=pl.CostEstimate(flops=4 * m_rows * KVH * keys * HD, bytes_accessed=4 * keys * KVH * HD, transcendentals=m_rows * KVH * keys),
    )(device, *arrays, *store, *extra)


def columns(rows):
    row = lax.broadcasted_iota(jnp.int32, (HD, HD), 0)
    square = jnp.zeros((HD, HD), jnp.float32)
    for i, x in enumerate(rows):
        square = jnp.where(row == i, jnp.broadcast_to(x, (HD, HD)), square)
    return square.T


def lse_rows(ref):
    tile = ref[BLOCK:PAYLOAD, :].astype(jnp.float32)
    return [tile[j:j + 1] + (tile[2 + j:3 + j] + tile[4 + j:5 + j]) for j in range(2)]


def shares(rows):
    top = functools.reduce(jnp.maximum, rows)
    w = [jnp.exp2(r - top) for r in rows]
    total = functools.reduce(jnp.add, w)
    inv = 1.0 / total
    return [x * inv for x in w], top + jnp.log2(total)


def pair_kernel(counts, own, *refs):
    kept, got = counts
    keeps, gots, outs = refs[:len(kept)], refs[len(kept):len(kept) + len(got)], refs[len(kept) + len(got):]
    places = [(keep, i) for keep, n in zip(keeps, kept) for i in range(n)]
    theirs_at = [ref.at[i] for ref, n in zip(gots, got) for i in range(n)]
    rows, lses = [], []
    for p, (keep, i) in enumerate(places):
        theirs = lse_rows(theirs_at[p])
        lses.append([])
        for j in range(2):
            w, lse = shares([keep[i, BLOCK + j:BLOCK + j + 1, :], theirs[j]])
            rows += w
            lses[-1].append(lse)
    cols = columns(rows)
    for p, (keep, i) in enumerate(places):
        for j in range(2):
            at, c = slice(j * HD, (j + 1) * HD), 4 * p + 2 * j
            acc = cols[:, c:c + 1] * keep[i, at, :] + cols[:, c + 1:c + 2] * theirs_at[p][at, :].astype(jnp.float32)
            outs[p][at, :] = acc.astype(outs[p].dtype)
            if own and p == 0:
                outs[p][BLOCK + j:BLOCK + j + 1, :] = lses[p][j]
        if not (own and p == 0):
            outs[p][BLOCK:PAYLOAD, :] = lse_tile(lses[p])


def pair(keeps, gots, own=False):
    counts = [k.shape[0] for k in keeps], [g.shape[0] for g in gots]
    shapes = [jax.ShapeDtypeStruct((PAYLOAD, HD), jnp.bfloat16)] * sum(counts[0])
    if own:
        shapes[0] = jax.ShapeDtypeStruct((KEPT, HD), jnp.float32)
    return pl.pallas_call(
        functools.partial(pair_kernel, counts, own),
        out_shape=shapes,
        in_specs=[VM] * (len(keeps) + len(gots)),
        out_specs=[VM] * len(shapes),
        compiler_params=limit(4),
    )(*keeps, *gots)


def final_kernel(n, own_ref, *refs):
    parts, out_ref = refs[:n], refs[n]
    theirs = [lse_rows(p) for p in parts]
    for j in range(2):
        at = slice(j * HD, (j + 1) * HD)
        w, _ = shares([own_ref[BLOCK + j:BLOCK + j + 1, :]] + [t[j] for t in theirs])
        cols = columns(w)
        acc = cols[:, 0:1] * own_ref[at, :]
        for i, p in enumerate(parts):
            acc = acc + cols[:, i + 1:i + 2] * p[at, :].astype(jnp.float32)
        out_ref[at, :] = acc.astype(jnp.bfloat16)


def final(own, parts):
    return pl.pallas_call(
        functools.partial(final_kernel, len(parts)),
        out_shape=jax.ShapeDtypeStruct((BLOCK, HD), jnp.bfloat16),
        in_specs=[VM] * (1 + len(parts)),
        out_specs=VM,
        compiler_params=limit(4),
        name="final",
    )(own, *parts)


def local(queries, new_keys, new_values, cache_keys, cache_values, cache_length, page_table):
    zsize = lax.axis_size("ctx") // 2
    half = zsize // 2

    def zshift(x, by):
        return lax.ppermute(x, "ctx", [(i, (i // zsize) * zsize + (i % zsize + by) % zsize) for i in range(2 * zsize)])

    def xswap(x):
        return lax.ppermute(x, "ctx", [(i, (i + zsize) % (2 * zsize)) for i in range(2 * zsize)])

    def blocks_at(k, base):
        return [((i, w), (base if w else 0) + i, (w, by)) for i, by in ((0, -k), (1, k)) for w in range(2)]

    device = lax.axis_index("ctx").astype(jnp.int32).reshape(1)
    mine = queries.reshape(ROWS, KVH * GROUP, HD).transpose(1, 0, 2).reshape(BLOCK, HD)
    entries = page_table.shape[0]
    meta = jnp.where(lax.iota(jnp.int32, entries + HD) < entries, jnp.pad(page_table, (0, HD)), cache_length[0]).reshape(1, -1)
    new = jnp.concatenate([new_keys, new_values])
    small = (NEWPAD, KVH * HD)
    keys, nk, nv = prep(prep_keys_kernel, device, [meta, new], cache_keys, [cache_keys.shape, small, small], 50)
    swapped, keys = lax.optimization_barrier((xswap(mine), keys))
    values, live = prep(prep_values_kernel, device, [meta], cache_values, [cache_values.shape, (cache_values.shape[0], HD)], 48)
    store = (keys, values, live, nk, nv)
    both = jnp.stack([mine, swapped])

    run = functools.partial(attend, zsize, device)
    up, down = both, both
    keeps, gots = [], []
    keep, send = run([both], [((0, w), 0, (w, 0)) for w in range(2)], store, 3)
    keeps.append(keep)
    for k in range(1, half):
        up, down, send = lax.optimization_barrier((zshift(up, 1), zshift(down, -1), send))
        if k == half - 1:
            far = zshift(up, 1)
        keep, send = run([up, down], blocks_at(k, 1 if k == 1 else 0), store, 3 if k == 1 else 2, send if k == 1 else None)
        keeps.append(keep)
        gots.append(xswap(send))
    far, send = lax.optimization_barrier((far, send))
    last_keep, send = run([far], [((0, w), 0, (w, half)) for w in range(2)], store, 1)
    last_got = xswap(send)

    third = pair(keeps[-1:], gots[-1:])
    own, *out = pair(keeps[:-1], gots[:-1], True)
    fourth = pair([last_keep], [last_got])
    back = [zshift(fourth[0], half), zshift(third[0], 1 - half), zshift(third[1], half - 1)]
    for k in range(half - 2, 0, -1):
        back += [zshift(out[2 * k - 2], -k), zshift(out[2 * k - 1], k)]
    out = final(own, back)
    return out.reshape(KVH * GROUP, ROWS, HD).transpose(1, 0, 2).reshape(ROWS, KVH * GROUP * HD)


def solution(mesh):
    spec = P(("req", "ctx"), None)
    in_specs = (spec, spec, spec, spec, spec, P("req"), P("req"))

    return jax.shard_map(local, mesh=mesh, in_specs=in_specs, out_specs=spec, check_vma=False)
```
